32 devices in a mesh: groups: 2 (over y), row: 4 (over x, core), col: 4 (over z).
Axes of the slice: x: 2, y: 2, z: 4, core: 2. Of those that a mesh axis runs over, the one named last changes fastest.
Arguments:
- right_sides: float32 [32, 16384], P(None, ('groups', 'row')), parts along dimension 1
- nugget: float32 [16384], P(('groups', 'row')), parts along dimension 0, may hold values from 1 to 4
- cov_blocks: bfloat16 [8, 4, 32, 256, 256], P(('groups', 'row'), 'col'), parts along dimension 0
- block_rows: int32 [8, 4, 32], P(('groups', 'row'), 'col'), parts along dimension 0, may hold values from 0 to 7, as said below
- block_cols: int32 [8, 4, 32], P(('groups', 'row'), 'col'), parts along dimension 0, may hold values from 0 to 7, as said below
- block_count: int32 [8, 4], P(('groups', 'row'), 'col'), parts along dimension 0, may hold values from 4 to 32, as said below
Outputs:
- solution: float32 [32, 16384], P(None, ('groups', 'row')), parts along dimension 1
- residual: float32 [32, 16384], P(None, ('groups', 'row')), parts along dimension 1
The draws below stay inside these ranges and needn't reach their ends.
There are 2 independent parts, one for each index of `groups`. The reference program is written for one: setup_inputs(seed, part) draws one part's arguments, and reference() takes and returns one part's arrays. A program takes and returns all parts, laid end to end along the dimension named above; each array names one. Nothing has to cross between parts.
Inputs may be any that keep to these rules, and one draw needn't show every extreme that they name: On each device the pairs (block_rows, block_cols) of all 32 slots are distinct; no stored block position of a problem is the mirror image of another (no pair is stored both as (g, h) and as (h, g)); on devices whose row and col index are equal, block_rows <= block_cols. `block_cols`: see block_rows. `block_count`: slots at or beyond the count are empty; some device of every problem has exactly 32 live slots.
All inputs are finite; a program needn't handle non-finite values.
Results may differ from the reference program's by a relative error of at most 0.0003.
Values sent between devices are 32-bit elements; how exact they have to be, the bound alone decides.
A program may use at most 64 MiB of HBM per device.

```python
import math
import jax
import jax.numpy as jnp
from jax import lax

BLOCK = 256
RHS = 32
BR = 8
SLOTS = 32
ITERS = 2
STATIONS = 8192
N_ROW = 4
N_COL = 4


def placed_pairs(key):
    base_key = jax.random.fold_in(key, 11)
    cell_total = BR * BR
    position = jnp.arange(cell_total, dtype=jnp.int32)
    local_row = position // BR
    local_col = position % BR
    row_ids = jnp.arange(N_ROW, dtype=jnp.int32)[:, None, None]
    col_ids = jnp.arange(N_COL, dtype=jnp.int32)[None, :, None]
    parity = (local_row + local_col) % 2
    usable = jnp.where(row_ids < col_ids, parity == 0, jnp.where(row_ids > col_ids, parity == 1, local_row <= local_col))
    scores = jax.random.randint(base_key, (N_ROW, N_COL, cell_total), 0, 4096, dtype=jnp.int32) * cell_total + position
    scores = jnp.where(usable, scores, scores + 4096 * cell_total)
    ranked = jnp.argsort(scores, axis=-1, stable=True)[..., :SLOTS].astype(jnp.int32)
    return (ranked // BR, ranked % BR)


def draw_block_rows(key, part):
    return placed_pairs(key)[0]


def draw_block_cols(key, part):
    return placed_pairs(key)[1]


def draw_block_count(key, part):
    key_one = jax.random.fold_in(key, 21)
    key_two = jax.random.fold_in(key, 22)
    key_three = jax.random.fold_in(key, 23)
    lowest = SLOTS // 8
    spread_range = SLOTS - lowest
    first_draw = jax.random.randint(key_one, (N_ROW, N_COL), 0, spread_range + 1, dtype=jnp.int32)
    second_draw = jax.random.randint(key_two, (N_ROW, N_COL), 0, spread_range + 1, dtype=jnp.int32)
    counts = lowest + first_draw * second_draw // max(spread_range, 1)
    full_device = jax.random.randint(key_three, (), 0, N_ROW * N_COL, dtype=jnp.int32)
    flat_ids = jnp.arange(N_ROW * N_COL, dtype=jnp.int32).reshape(N_ROW, N_COL)
    return jnp.where(flat_ids == full_device, SLOTS, counts).astype(jnp.int32)


def draw_cov_blocks(key, part):
    base_key = jax.random.fold_in(key, 31)
    spread_scale = 0.3 * (2.0 * N_COL * SLOTS * BLOCK / BR) ** (-0.5)
    shape_all = (N_ROW, N_COL, SLOTS, BLOCK, BLOCK)
    noise_part = jax.random.normal(base_key, shape_all, jnp.float32)
    return (spread_scale * noise_part).astype(jnp.bfloat16)


def draw_right_sides(key, part):
    base_key = jax.random.fold_in(key, 41)
    ramped = 1.0 + 2.0 * jnp.arange(STATIONS, dtype=jnp.float32) / (STATIONS - 1)
    noise_part = jax.random.normal(base_key, (RHS, STATIONS), jnp.float32)
    return jnp.clip(noise_part, -6.0, 6.0) * ramped[None, :]


def block_scale(rng, dims, shards, smallest, largest):
    def one(dim, parts):
        heights = jax.random.uniform(jax.random.fold_in(jax.random.fold_in(rng, 6), dim), (parts,), jnp.float32, smallest / len(shards), largest / len(shards))
        return jnp.repeat(jnp.exp(heights), dims[dim] // parts).reshape((-1,) + (1,) * (len(dims) - dim - 1))

    loudness = one(*shards[0])
    for cut in shards[1:]:
        loudness = loudness * one(*cut)
    return loudness


def setup_inputs(seed: int = 0, part: int = 0) -> dict:
    arg_keys = jax.random.split(jax.random.key(seed), 7)
    part_keys = jax.random.split(jax.random.fold_in(arg_keys[6], part), 7)
    return {
        "right_sides": draw_right_sides(jax.random.fold_in(jax.random.fold_in(arg_keys[6], part), 71), part),
        "nugget": jnp.clip(jnp.exp(math.log(4.0) - 1.3862944 * jax.random.uniform(part_keys[1], (STATIONS,), jnp.float32) ** block_scale(part_keys[1], (STATIONS,), ((0, 4),), -0.2, 0.2)), 1.0, 4.0),
        "cov_blocks": draw_cov_blocks(jax.random.fold_in(jax.random.fold_in(arg_keys[6], part), 71), part),
        "block_rows": draw_block_rows(jax.random.fold_in(jax.random.fold_in(arg_keys[6], part), 71), part),
        "block_cols": draw_block_cols(jax.random.fold_in(jax.random.fold_in(arg_keys[6], part), 71), part),
        "block_count": draw_block_count(jax.random.fold_in(jax.random.fold_in(arg_keys[6], part), 71), part),
    }


def apply_cov(field, nugget, cov_blocks, block_rows, block_cols, block_count):
    tile_count = STATIONS // BLOCK
    tile_view = field.reshape(RHS, tile_count, BLOCK)
    col_ids = jnp.arange(N_COL, dtype=jnp.int32)
    slot_ids = jnp.arange(SLOTS, dtype=jnp.int32)

    def row_update(summed, items):
        row_index, blocks, slot_rows, slot_cols, live_count = items
        live_weight = (slot_ids[None, :] < live_count[:, None]).astype(jnp.float32).reshape(-1)
        glob_rows = (row_index * BR + slot_rows).reshape(-1).astype(jnp.int32)
        glob_cols = (col_ids[:, None] * BR + slot_cols).reshape(-1).astype(jnp.int32)
        matrices = blocks.reshape(N_COL * SLOTS, BLOCK, BLOCK).astype(jnp.float32)
        direct = jnp.einsum("rmk,mjk->rmj", tile_view[:, glob_cols], matrices,
                            precision=lax.Precision.HIGHEST) * live_weight[None, :, None]
        mirror = jnp.einsum("rmj,mjk->rmk", tile_view[:, glob_rows], matrices,
                            precision=lax.Precision.HIGHEST) * live_weight[None, :, None]
        summed = summed.at[:, glob_rows].add(direct)
        summed = summed.at[:, glob_cols].add(mirror)
        return summed, None

    empty_sum = jnp.zeros((RHS, tile_count, BLOCK), jnp.float32)
    summed, _ = lax.scan(row_update, empty_sum,
                         (jnp.arange(N_ROW, dtype=jnp.int32), cov_blocks, block_rows, block_cols, block_count))
    return nugget[None, :] * field + summed.reshape(RHS, STATIONS)


def reference(right_sides, nugget, cov_blocks, block_rows, block_cols, block_count):
    solution = jnp.zeros_like(right_sides)
    residual = right_sides
    direction = right_sides
    norm_now = jnp.sum(residual * residual, axis=1)
    for turn_index in range(ITERS):
        applied = apply_cov(direction, nugget, cov_blocks, block_rows, block_cols, block_count)
        step_size = norm_now / jnp.sum(direction * applied, axis=1)
        solution = solution + step_size[:, None] * direction
        residual = residual - step_size[:, None] * applied
        norm_next = jnp.sum(residual * residual, axis=1)
        direction = residual + (norm_next / norm_now)[:, None] * direction
        norm_now = norm_next
    return solution, residual
```

```python
import functools

import jax
import jax.numpy as jnp
from jax import lax
from jax.experimental import pallas as pl
from jax.experimental.pallas import tpu as pltpu
from jax.sharding import PartitionSpec as P

ITERS = 2
LANES = 128
CORES = 2
PIECES = 3
UNROLL = 8


def kernel(
    n_row, n_col,
    cols_ref, rows_ref, pos_ref, rhs_ref, nugget_ref, stored_ref,
    solution_ref, residual_ref,
    blocks, vec, far, near_x, far_x, products, direct, mirror,
    m_part, m_half, m_root, rs_in, r_one, p_one, ex_out, ex_in,
    block_sem, far_send, far_recv, fwd_send, mp_send, mp_recv, mr_send, mr_recv,
    rs_send, rs_recv, ag_send, ag_recv, ex_send, ex_recv,
):
    groups, series, _ = vec.shape[1:]
    slots, tile, _ = blocks.shape
    tiles = near_x.shape[0]
    per_tile = tile // LANES
    chunk = groups // n_col
    chips = n_row // CORES
    half_rows = series // CORES
    me_row = lax.axis_index("row")
    me_col = lax.axis_index("col")
    chip, core = me_row // CORES, lax.rem(me_row, CORES)
    partner = chip * CORES + (1 - core)
    root = me_col
    root_chip = root // CORES
    is_root = me_row == root
    on_root_chip = chip == root_chip
    is_root_partner = jnp.logical_and(on_root_chip, jnp.logical_not(is_root))
    away = jnp.logical_not(on_root_chip)
    finals = []

    def copy(src, dst, send_sem, recv_sem, **where):
        return pltpu.make_async_remote_copy(
            src_ref=src, dst_ref=dst, send_sem=send_sem, recv_sem=recv_sem,
            device_id=where, device_id_type=pl.DeviceIdType.MESH)

    def arrived(dst, recv_sem, send_sem):
        copy(dst, dst, send_sem, recv_sem, row=partner).wait_recv()

    def own_half(ref, which):
        return ref.at[:, pl.ds(pl.multiple_of(which * half_rows, half_rows), half_rows), :]

    def part(k):
        return pl.ds(k * chunk, chunk)

    barrier = pltpu.get_barrier_semaphore()
    for j in range(1, n_row):
        pl.semaphore_signal(barrier, inc=1, device_id={"row": lax.rem(me_row + j, n_row)},
                            device_id_type=pl.DeviceIdType.MESH)
    for j in range(1, n_col):
        pl.semaphore_signal(barrier, inc=1, device_id={"col": lax.rem(me_col + j, n_col)},
                            device_id_type=pl.DeviceIdType.MESH)
    fetch = pltpu.make_async_copy(stored_ref, blocks, block_sem)
    fetch.start()

    def split_into(dst, src):
        def one(t, carry):
            whole = jnp.concatenate([src[t * per_tile + k] for k in range(per_tile)], axis=1)
            rest = whole
            for piece in range(PIECES):
                top = rest.astype(jnp.bfloat16)
                dst[t, piece * series:(piece + 1) * series, :] = top
                rest = rest - top.astype(jnp.float32)
            return carry
        lax.fori_loop(0, tiles, one, 0)

    def multiply(pick_ref, x_ref, contract):
        def some(step, carry):
            for k in range(UNROLL):
                s = step * UNROLL + k
                out = lax.dot_general(x_ref[pick_ref[s]], blocks[s],
                                      (((1,), (contract,)), ((), ())),
                                      preferred_element_type=jnp.float32)
                total = out[(PIECES - 1) * series:]
                for piece in range(PIECES - 2, -1, -1):
                    total = total + out[piece * series:(piece + 1) * series]
                products[s] = total
            return carry
        lax.fori_loop(0, slots // UNROLL, some, 0)

    def collect(dst, by_row):
        def one(t, carry):
            total = None
            for k in range(tiles):
                term = products[pos_ref[t * tiles + k] if by_row else pos_ref[k * tiles + t]]
                total = term if total is None else total + term
            for k in range(per_tile):
                dst[t * per_tile + k] = total[:, k * LANES:(k + 1) * LANES]
            return carry
        lax.fori_loop(0, tiles, one, 0)

    def dot(left, right):
        def one(g, total):
            return total + left(g) * right(g)
        return lax.fori_loop(0, groups, one, jnp.zeros((series, LANES), jnp.float32), unroll=4)

    def exchange_start(k, parts):
        for q, value in enumerate(parts):
            ex_out[k, q] = value
        count = len(parts)
        for j in range(1, n_row):
            c = copy(ex_out.at[k, pl.ds(0, count)], ex_in.at[k, j - 1, pl.ds(0, count)],
                     ex_send.at[k, j - 1], ex_recv.at[k, j - 1],
                     row=lax.rem(me_row + j, n_row))
            c.start()
            finals.append(c.wait_send)

    def exchange_done(k, count):
        for j in range(1, n_row):
            arrived(ex_in.at[k, j - 1, pl.ds(0, count)], ex_recv.at[k, j - 1], ex_send.at[k, j - 1])
        sums = []
        for q in range(count):
            total = ex_out[k, q]
            for j in range(1, n_row):
                total = total + ex_in[k, j - 1, q]
            sums.append(jnp.sum(total, axis=1, keepdims=True))
        return sums

    def far_start(i):
        for j in range(1, chips):
            for h in range(CORES):
                c = copy(own_half(vec.at[i], h), own_half(far.at[i], h),
                         far_send.at[i, j, h], far_recv.at[i, h],
                         row=lax.rem(root_chip + j, chips) * CORES + h)
                pl.when(is_root)(c.start)
                finals.append(lambda c=c: pl.when(is_root)(c.wait_send))
        for h in range(CORES):
            c = copy(own_half(vec.at[i], h), own_half(far.at[i], h),
                     far_send.at[i, 0, h], far_recv.at[i, h], row=partner)
            pl.when(is_root)(c.start)
            finals.append(lambda c=c: pl.when(is_root)(c.wait_send))

    def far_relay(i):
        def go():
            mine = own_half(far.at[i], core)
            arrived(mine, far_recv.at[i, core], fwd_send.at[i])
            copy(mine, mine, fwd_send.at[i], far_recv.at[i, core], row=partner).start()
        pl.when(away)(go)
        mine = own_half(far.at[i], core)
        c = copy(mine, mine, fwd_send.at[i], far_recv.at[i, core], row=partner)
        finals.append(lambda: pl.when(away)(c.wait_send))

    def far_done(i):
        def last():
            arrived(own_half(far.at[i], 1 - core), far_recv.at[i, 1 - core], fwd_send.at[i])
        def both():
            for h in range(CORES):
                arrived(own_half(far.at[i], h), far_recv.at[i, h], fwd_send.at[i])
        pl.when(away)(last)
        pl.when(is_root_partner)(both)
        pl.when(is_root)(lambda: split_into(far_x, vec.at[i]))
        pl.when(jnp.logical_not(is_root))(lambda: split_into(far_x, far.at[i]))

    def mirror_start(i):
        other = copy(own_half(mirror.at[i], 1 - core), m_part.at[i], mp_send.at[i], mp_recv.at[i], row=partner)
        whole = copy(mirror.at[i], m_root.at[i, chips - 1], mp_send.at[i],
                     mr_recv.at[i, chips - 1, 0], row=root)
        pl.when(away)(other.start)
        pl.when(is_root_partner)(whole.start)
        finals.append(lambda: pl.when(away)(other.wait_send))
        finals.append(lambda: pl.when(is_root_partner)(whole.wait_send))

    def mirror_relay(i):
        slot = lax.rem(chip - root_chip + chips, chips) - 1
        slot = jnp.maximum(slot, 0)
        onward = copy(m_half.at[i], own_half(m_root.at[i, slot], core), mr_send.at[i],
                      mr_recv.at[i, slot, core], row=root)
        def go():
            arrived(m_part.at[i], mp_recv.at[i], mp_send.at[i])
            first = pl.multiple_of(core * half_rows, half_rows)
            def one(g, carry):
                m_half[i, g] = mirror[i, g, pl.ds(first, half_rows), :] + m_part[i, g]
                return carry
            lax.fori_loop(0, groups, one, 0, unroll=4)
            onward.start()
        pl.when(away)(go)
        finals.append(lambda: pl.when(away)(onward.wait_send))

    def mirror_done(i):
        def go():
            for j in range(chips - 1):
                for h in range(CORES):
                    arrived(own_half(m_root.at[i, j], h), mr_recv.at[i, j, h], mr_send.at[i])
            arrived(m_root.at[i, chips - 1], mr_recv.at[i, chips - 1, 0], mr_send.at[i])
            def one(g, carry):
                total = direct[i, g] + mirror[i, g]
                for j in range(chips):
                    total = total + m_root[i, j, g]
                direct[i, g] = total
                return carry
            lax.fori_loop(0, groups, one, 0, unroll=2)
        pl.when(is_root)(go)

    def reduce_start(i):
        for j in range(n_col - 1, 0, -1):
            to = lax.rem(me_col + j, n_col)
            c = copy(direct.at[i, part(to)], rs_in.at[i, j - 1], rs_send.at[i, j - 1],
                     rs_recv.at[i, j - 1], col=to)
            c.start()
            finals.append(c.wait_send)

    def reduce_done(i):
        for j in range(1, n_col):
            arrived(rs_in.at[i, j - 1], rs_recv.at[i, j - 1], rs_send.at[i, j - 1])
        for k in range(chunk):
            g = me_col * chunk + k
            total = direct[i, g] + nugget_ref[pl.ds(g, 1), :] * vec[i, g]
            for j in range(1, n_col):
                total = total + rs_in[i, j - 1, k]
            vec[i + 1, g] = total

    def gather_start(i):
        mine = vec.at[i + 1, part(me_col)]
        for j in range(n_col - 1, 0, -1):
            c = copy(mine, mine, ag_send.at[i, j - 1], ag_recv.at[i, j - 1],
                     col=lax.rem(me_col + j, n_col))
            c.start()
            finals.append(c.wait_send)

    def gather_done(i):
        for j in range(1, n_col):
            arrived(vec.at[i + 1, part(lax.rem(me_col - j + n_col, n_col))],
                    ag_recv.at[i, j - 1], ag_send.at[i, j - 1])

    for g in range(groups):
        vec[0, g] = rhs_ref[:, g * LANES:(g + 1) * LANES]
    split_into(near_x, vec.at[0])
    products[slots] = jnp.zeros((series, tile), jnp.float32)
    pl.semaphore_wait(barrier, n_row - 1 + n_col - 1)

    for i in range(ITERS):
        far_start(i)
        if i == 1:
            exchange_start(0, [dot(lambda g: vec[0, g], lambda g: vec[0, g]),
                               dot(lambda g: vec[0, g], lambda g: vec[1, g])])
            split_into(near_x, vec.at[1])
        else:
            fetch.wait()
        multiply(rows_ref, near_x, 0)
        collect(mirror.at[i], False)
        mirror_start(i)
        far_relay(i)
        mirror_relay(i)
        far_done(i)
        multiply(cols_ref, far_x, 1)
        collect(direct.at[i], True)
        mirror_done(i)
        reduce_start(i)
        if i == 1:
            norm_now, curvature = exchange_done(0, 2)
            alpha0 = norm_now / curvature
            def leave(g, total):
                left = vec[0, g] - alpha0 * vec[1, g]
                r_one[g] = left
                return total + left * left
            partial = lax.fori_loop(0, groups, leave, jnp.zeros((series, LANES), jnp.float32))
            exchange_start(1, [partial])
        reduce_done(i)
        gather_start(i)
        if i == 1:
            (norm_next,) = exchange_done(1, 1)
            beta0 = norm_next / norm_now
            def turn(g, carry):
                p_one[g] = r_one[g] + beta0 * vec[0, g]
                return carry
            lax.fori_loop(0, groups, turn, 0)
        gather_done(i)

    def image(g):
        return vec[1, g] + beta0 * vec[1, g] - alpha0 * vec[2, g]
    exchange_start(2, [dot(image, lambda g: p_one[g])])
    (curvature1,) = exchange_done(2, 1)
    alpha1 = norm_next / curvature1
    for g in range(groups):
        lanes = slice(g * LANES, (g + 1) * LANES)
        solution_ref[:, lanes] = alpha0 * vec[0, g] + alpha1 * p_one[g]
        residual_ref[:, lanes] = r_one[g] - alpha1 * image(g)
    for wait in finals:
        wait()


def on_device(n_row, n_col, right_sides, nugget, cov_blocks, block_rows, block_cols, block_count):
    slots, tile = cov_blocks.shape[2:4]
    series, width = right_sides.shape
    tiles = width // tile
    groups = width // LANES
    chunk = groups // n_col
    chips = n_row // CORES
    rows, cols = block_rows[0, 0], block_cols[0, 0]
    slot_ids = jnp.arange(slots, dtype=jnp.int32)
    cell = jnp.where(slot_ids < block_count[0, 0], rows * tiles + cols, -1)
    cells = jnp.arange(tiles * tiles, dtype=jnp.int32)
    found = jnp.where(cell[None, :] == cells[:, None], slots - slot_ids[None, :], 0)
    pos = slots - jnp.max(found, axis=1)

    f32 = jnp.float32
    field = (groups, series, LANES)
    half = (groups, series // CORES, LANES)
    dma = pltpu.SemaphoreType.DMA
    smem = pl.BlockSpec(memory_space=pltpu.SMEM)
    vmem = pl.BlockSpec(memory_space=pltpu.VMEM)
    return pl.pallas_call(
        functools.partial(kernel, n_row, n_col),
        out_shape=(jax.ShapeDtypeStruct((series, width), f32),) * 2,
        in_specs=[smem, smem, smem, vmem, vmem, pl.BlockSpec(memory_space=pl.ANY)],
        out_specs=(vmem, vmem),
        scratch_shapes=[
            pltpu.VMEM((slots, tile, tile), jnp.bfloat16),
            pltpu.VMEM((ITERS + 1,) + field, f32),
            pltpu.VMEM((ITERS,) + field, f32),
            pltpu.VMEM((tiles, PIECES * series, tile), jnp.bfloat16),
            pltpu.VMEM((tiles, PIECES * series, tile), jnp.bfloat16),
            pltpu.VMEM((slots + 1, series, tile), f32),
            pltpu.VMEM((ITERS,) + field, f32),
            pltpu.VMEM((ITERS,) + field, f32),
            pltpu.VMEM((ITERS,) + half, f32),
            pltpu.VMEM((ITERS,) + half, f32),
            pltpu.VMEM((ITERS, chips) + field, f32),
            pltpu.VMEM((ITERS, n_col - 1, chunk, series, LANES), f32),
            pltpu.VMEM(field, f32),
            pltpu.VMEM(field, f32),
            pltpu.VMEM((3, 2, series, LANES), f32),
            pltpu.VMEM((3, n_row - 1, 2, series, LANES), f32),
            dma,
            dma((ITERS, chips, CORES)), dma((ITERS, CORES)), dma((ITERS,)),
            dma((ITERS,)), dma((ITERS,)), dma((ITERS,)), dma((ITERS, chips, CORES)),
            dma((ITERS, n_col - 1)), dma((ITERS, n_col - 1)),
            dma((ITERS, n_col - 1)), dma((ITERS, n_col - 1)),
            dma((3, n_row - 1)), dma((3, n_row - 1)),
        ],
        compiler_params=pltpu.CompilerParams(collective_id=0, has_side_effects=True),
    )(cols, rows, pos, right_sides, nugget.reshape(groups, LANES), cov_blocks[0, 0])


def solution(mesh):
    placed = (
        P(None, ("groups", "row")),
        P(("groups", "row")),
        P(("groups", "row"), "col", None, None, None),
        P(("groups", "row"), "col", None),
        P(("groups", "row"), "col", None),
        P(("groups", "row"), "col"),
    )
    return jax.shard_map(
        functools.partial(on_device, mesh.shape["row"], mesh.shape["col"]),
        mesh=mesh,
        in_specs=placed,
        out_specs=(P(None, ("groups", "row")), P(None, ("groups", "row"))),
        check_vma=False,
    )
```

```python
import functools

import jax
import jax.numpy as jnp
from jax import lax
from jax.experimental import pallas as pl
from jax.experimental.pallas import tpu as pltpu
from jax.sharding import PartitionSpec as P

ITERS = 2
LANES = 128
CORES = 2
PIECES = 3
UNROLL = 8
BATCHES = 2


def kernel(
    n_row, n_col,
    cols_ref, rows_ref, pos_ref, rhs_ref, nugget_ref, stored_ref,
    start_ref, p_ref, r_ref, image_ref, step_ref,
    blocks, turned, vec, far, near_x, far_x, products, direct, mirror,
    m_part, m_half, m_root, rs_in, r_one, p_one, ex_out, ex_in,
    block_sem, far_send, far_recv, fwd_send, mp_send, mp_recv, mr_send, mr_recv,
    rs_send, rs_recv, ag_send, ag_recv, ex_send, ex_recv,
):
    batches, groups, series, _ = vec.shape[1:]
    slots, tile, _ = blocks.shape
    tiles = near_x.shape[1]
    per_tile = tile // LANES
    chunk = groups // n_col
    chips = n_row // CORES
    half_groups = groups // CORES
    me_row = lax.axis_index("row")
    me_col = lax.axis_index("col")
    chip, core = me_row // CORES, lax.rem(me_row, CORES)
    partner = chip * CORES + (1 - core)
    root = me_col
    root_chip = root // CORES
    is_root = me_row == root
    on_root_chip = chip == root_chip
    is_root_partner = jnp.logical_and(on_root_chip, jnp.logical_not(is_root))
    away = jnp.logical_not(on_root_chip)
    finals = []

    def copy(src, dst, send_sem, recv_sem, **where):
        return pltpu.make_async_remote_copy(
            src_ref=src, dst_ref=dst, send_sem=send_sem, recv_sem=recv_sem,
            device_id=where, device_id_type=pl.DeviceIdType.MESH)

    def arrived(dst, recv_sem, send_sem):
        copy(dst, dst, send_sem, recv_sem, row=partner).wait_recv()

    def own_half(ref, which):
        return ref.at[pl.ds(which * half_groups, half_groups)]

    def part(k):
        return pl.ds(k * chunk, chunk)

    barrier = pltpu.get_barrier_semaphore()
    for j in range(1, n_row):
        pl.semaphore_signal(barrier, inc=1, device_id={"row": lax.rem(me_row + j, n_row)},
                            device_id_type=pl.DeviceIdType.MESH)
    for j in range(1, n_col):
        pl.semaphore_signal(barrier, inc=1, device_id={"col": lax.rem(me_col + j, n_col)},
                            device_id_type=pl.DeviceIdType.MESH)
    fetch = pltpu.make_async_copy(stored_ref, blocks, block_sem)
    fetch.start()

    def split_into(dst, src):
        def one(t, carry):
            rest = jnp.concatenate([src[t * per_tile + k] for k in range(per_tile)], axis=1)
            tops = []
            for piece in range(PIECES):
                tops.append(rest.astype(jnp.bfloat16).astype(jnp.float32))
                rest = rest - tops[-1]
            dst[t] = jnp.concatenate(tops, axis=0).astype(jnp.bfloat16)
            return carry
        lax.fori_loop(0, tiles, one, 0)

    def multiply(pick_ref, x_ref, matrices):
        def some(step, carry):
            for k in range(UNROLL):
                s = step * UNROLL + k
                out = jnp.dot(x_ref[pick_ref[s]], matrices[s], preferred_element_type=jnp.float32)
                total = out[(PIECES - 1) * series:]
                for piece in range(PIECES - 2, -1, -1):
                    total = total + out[piece * series:(piece + 1) * series]
                products[s] = total
            return carry
        lax.fori_loop(0, slots // UNROLL, some, 0)

    def collect(dst, by_row):
        def one(t, carry):
            total = None
            for k in range(tiles):
                term = products[pos_ref[t * tiles + k] if by_row else pos_ref[k * tiles + t]]
                total = term if total is None else total + term
            for k in range(per_tile):
                dst[t * per_tile + k] = total[:, k * LANES:(k + 1) * LANES]
            return carry
        lax.fori_loop(0, tiles, one, 0)

    def dot(left, right):
        def one(g, total):
            return total + left(g) * right(g)
        return lax.fori_loop(0, groups, one, jnp.zeros((series, LANES), jnp.float32), unroll=4)

    def used(k):
        return pl.ds(0, 2 if k == 0 else 1)

    def exchange_start(k):
        for j in range(1, n_row):
            c = copy(ex_out.at[k, used(k)], ex_in.at[k, j - 1, used(k)], ex_send.at[k, j - 1], ex_recv.at[k, j - 1],
                     row=lax.rem(me_row + j, n_row))
            c.start()
            finals.append(c.wait_send)

    def exchange_done(k):
        for j in range(1, n_row):
            arrived(ex_in.at[k, j - 1, used(k)], ex_recv.at[k, j - 1], ex_send.at[k, j - 1])

    def exchanged(k, q, b):
        total = ex_out[k, q, b]
        for j in range(1, n_row):
            total = total + ex_in[k, j - 1, q, b]
        return jnp.sum(total, axis=1, keepdims=True)

    def far_start(i, b):
        for j in range(1, chips):
            for h in range(CORES):
                c = copy(own_half(vec.at[i, b], h), own_half(far.at[i, b], h),
                         far_send.at[i, b, j, h], far_recv.at[i, b, h],
                         row=lax.rem(root_chip + j, chips) * CORES + h)
                pl.when(is_root)(c.start)
                finals.append(lambda c=c: pl.when(is_root)(c.wait_send))
        for h in range(CORES):
            c = copy(own_half(vec.at[i, b], h), own_half(far.at[i, b], h),
                     far_send.at[i, b, 0, h], far_recv.at[i, b, h], row=partner)
            pl.when(is_root)(c.start)
            finals.append(lambda c=c: pl.when(is_root)(c.wait_send))

    def far_relay(i, b):
        def go():
            mine = own_half(far.at[i, b], core)
            arrived(mine, far_recv.at[i, b, core], fwd_send.at[i, b])
            copy(mine, mine, fwd_send.at[i, b], far_recv.at[i, b, core], row=partner).start()
        pl.when(away)(go)
        mine = own_half(far.at[i, b], core)
        c = copy(mine, mine, fwd_send.at[i, b], far_recv.at[i, b, core], row=partner)
        finals.append(lambda: pl.when(away)(c.wait_send))

    def far_done(i, b):
        def last():
            arrived(own_half(far.at[i, b], 1 - core), far_recv.at[i, b, 1 - core], fwd_send.at[i, b])
        def both():
            for h in range(CORES):
                arrived(own_half(far.at[i, b], h), far_recv.at[i, b, h], fwd_send.at[i, b])
        pl.when(away)(last)
        pl.when(is_root_partner)(both)
        pl.when(is_root)(lambda: split_into(far_x.at[b], vec.at[i, b]))
        pl.when(jnp.logical_not(is_root))(lambda: split_into(far_x.at[b], far.at[i, b]))

    def mirror_start(i, b):
        other = copy(own_half(mirror.at[i, b], 1 - core), m_part.at[i, b], mp_send.at[i, b], mp_recv.at[i, b], row=partner)
        whole = copy(mirror.at[i, b], m_root.at[i, b, chips - 1], mp_send.at[i, b],
                     mr_recv.at[i, b, chips - 1, 0], row=root)
        pl.when(away)(other.start)
        pl.when(is_root_partner)(whole.start)
        finals.append(lambda: pl.when(away)(other.wait_send))
        finals.append(lambda: pl.when(is_root_partner)(whole.wait_send))

    def mirror_relay(i, b):
        slot = lax.rem(chip - root_chip + chips, chips) - 1
        slot = jnp.maximum(slot, 0)
        onward = copy(m_half.at[i, b], own_half(m_root.at[i, b, slot], core), mr_send.at[i, b],
                      mr_recv.at[i, b, slot, core], row=root)
        def go():
            arrived(m_part.at[i, b], mp_recv.at[i, b], mp_send.at[i, b])
            first = core * half_groups
            def one(g, carry):
                m_half[i, b, g] = mirror[i, b, first + g] + m_part[i, b, g]
                return carry
            lax.fori_loop(0, half_groups, one, 0, unroll=4)
            onward.start()
        pl.when(away)(go)
        finals.append(lambda: pl.when(away)(onward.wait_send))

    def mirror_done(i, b):
        def go():
            for j in range(chips - 1):
                for h in range(CORES):
                    arrived(own_half(m_root.at[i, b, j], h), mr_recv.at[i, b, j, h], mr_send.at[i, b])
            arrived(m_root.at[i, b, chips - 1], mr_recv.at[i, b, chips - 1, 0], mr_send.at[i, b])
            def one(g, carry):
                total = direct[i, b, g] + mirror[i, b, g]
                for j in range(chips):
                    total = total + m_root[i, b, j, g]
                direct[i, b, g] = total
                return carry
            lax.fori_loop(0, groups, one, 0, unroll=2)
        pl.when(is_root)(go)

    def reduce_start(i, b):
        for j in range(n_col - 1, 0, -1):
            to = lax.rem(me_col + j, n_col)
            c = copy(direct.at[i, b, part(to)], rs_in.at[i, b, j - 1], rs_send.at[i, b, j - 1],
                     rs_recv.at[i, b, j - 1], col=to)
            c.start()
            finals.append(c.wait_send)

    def reduce_done(i, b):
        for j in range(1, n_col):
            arrived(rs_in.at[i, b, j - 1], rs_recv.at[i, b, j - 1], rs_send.at[i, b, j - 1])
        for k in range(chunk):
            g = me_col * chunk + k
            total = direct[i, b, g] + nugget_ref[pl.ds(g, 1), :] * vec[i, b, g]
            for j in range(1, n_col):
                total = total + rs_in[i, b, j - 1, k]
            vec[i + 1, b, g] = total

    def gather_start(i, b):
        mine = vec.at[i + 1, b, part(me_col)]
        for j in range(n_col - 1, 0, -1):
            c = copy(mine, mine, ag_send.at[i, b, j - 1], ag_recv.at[i, b, j - 1],
                     col=lax.rem(me_col + j, n_col))
            c.start()
            finals.append(c.wait_send)

    def gather_done(i, b):
        for j in range(1, n_col):
            arrived(vec.at[i + 1, b, part(lax.rem(me_col - j + n_col, n_col))],
                    ag_recv.at[i, b, j - 1], ag_send.at[i, b, j - 1])

    for b in range(batches):
        rows = slice(b * series, (b + 1) * series)
        for g in range(groups):
            vec[0, b, g] = rhs_ref[rows, g * LANES:(g + 1) * LANES]
    pl.semaphore_wait(barrier, n_row - 1 + n_col - 1)
    for b in range(batches):
        far_start(0, b)
    products[slots] = jnp.zeros((series, tile), jnp.float32)

    def mirror_part(i, b):
        split_into(near_x.at[b], vec.at[i, b])
        if i == 0 and b == 0:
            fetch.wait()
        multiply(rows_ref, near_x.at[b], blocks)
        collect(mirror.at[i, b], False)

    def relay_part(i, b):
        mirror_relay(i, b)
        far_relay(i, b)

    def direct_part(i, b):
        far_done(i, b)
        multiply(cols_ref, far_x.at[b], turned)
        collect(direct.at[i, b], True)
        mirror_done(i, b)
        reduce_start(i, b)

    def middle(i):
        relay_part(i, 0)
        for b in range(batches):
            if b + 1 < batches:
                relay_part(i, b + 1)
            if i == 0 and b == 0:
                lax.fori_loop(slots // 2, slots, transpose, 0, unroll=4)
            direct_part(i, b)

    for b in range(batches):
        mirror_part(0, b)
    for b in range(batches):
        mirror_start(0, b)
    def transpose(s, carry):
        turned[s] = blocks[s].T
        return carry
    lax.fori_loop(0, slots // 2, transpose, 0, unroll=4)
    middle(0)
    for b in range(batches):
        reduce_done(0, b)
        gather_start(0, b)
    for b in range(batches):
        ex_out[0, 0, b] = dot(lambda g: vec[0, b, g], lambda g: vec[0, b, g])
    for b in range(batches):
        gather_done(0, b)
        far_start(1, b)
        mirror_part(1, b)
        mirror_start(1, b)
        ex_out[0, 1, b] = dot(lambda g: vec[0, b, g], lambda g: vec[1, b, g])
    exchange_start(0)
    middle(1)
    exchange_done(0)
    norm_now = [exchanged(0, 0, b) for b in range(batches)]
    alpha0 = [norm_now[b] / exchanged(0, 1, b) for b in range(batches)]
    for b in range(batches):
        def leave(g, total):
            left = vec[0, b, g] - alpha0[b] * vec[1, b, g]
            r_one[b, g] = left
            return total + left * left
        ex_out[1, 0, b] = lax.fori_loop(0, groups, leave, jnp.zeros((series, LANES), jnp.float32))
    exchange_start(1)
    for b in range(batches):
        reduce_done(1, b)
        gather_start(1, b)
    exchange_done(1)
    norm_next = [exchanged(1, 0, b) for b in range(batches)]
    beta0 = [norm_next[b] / norm_now[b] for b in range(batches)]
    for b in range(batches):
        def turn(g, carry):
            p_one[b, g] = r_one[b, g] + beta0[b] * vec[0, b, g]
            return carry
        lax.fori_loop(0, groups, turn, 0)

    def image(b, g):
        return vec[1, b, g] + beta0[b] * vec[1, b, g] - alpha0[b] * vec[2, b, g]
    for b in range(batches):
        gather_done(1, b)
        ex_out[2, 0, b] = dot(lambda g: image(b, g), lambda g: p_one[b, g])
    exchange_start(2)
    for b in range(batches):
        rows = slice(b * series, (b + 1) * series)
        for g in range(groups):
            lanes = slice(g * LANES, (g + 1) * LANES)
            start_ref[rows, lanes] = alpha0[b] * vec[0, b, g]
            p_ref[rows, lanes] = p_one[b, g]
            r_ref[rows, lanes] = r_one[b, g]
            image_ref[rows, lanes] = image(b, g)
    exchange_done(2)
    for b in range(batches):
        rows = slice(b * series, (b + 1) * series)
        alpha1 = norm_next[b] / exchanged(2, 0, b)
        step_ref[rows, :] = jnp.broadcast_to(alpha1, (series, groups * LANES))
    for wait in finals:
        wait()


def on_device(n_row, n_col, right_sides, nugget, cov_blocks, block_rows, block_cols, block_count):
    slots, tile = cov_blocks.shape[2:4]
    series, width = right_sides.shape
    tiles = width // tile
    groups = width // LANES
    chunk = groups // n_col
    chips = n_row // CORES
    rows, cols = block_rows[0, 0], block_cols[0, 0]
    slot_ids = jnp.arange(slots, dtype=jnp.int32)
    cells = jnp.arange(tiles * tiles, dtype=jnp.int32)[:, None]
    live = slot_ids[None, :] < block_count
    here = jnp.logical_and(rows[None, :] * tiles + cols[None, :] == cells, live)
    pos = jnp.min(jnp.where(here, slot_ids[None, :], slots), axis=1)

    f32 = jnp.float32
    batch = series // BATCHES
    runs = (ITERS, BATCHES)
    field = (groups, batch, LANES)
    half = (groups // CORES, batch, LANES)
    dma = pltpu.SemaphoreType.DMA
    smem = pl.BlockSpec(memory_space=pltpu.SMEM)
    vmem = pl.BlockSpec(memory_space=pltpu.VMEM)
    start, turn, left, image, step = pl.pallas_call(
        functools.partial(kernel, n_row, n_col),
        out_shape=(jax.ShapeDtypeStruct((series, width), f32),) * 5,
        in_specs=[smem, smem, smem, vmem, vmem, pl.BlockSpec(memory_space=pl.ANY)],
        out_specs=(vmem,) * 5,
        scratch_shapes=[
            pltpu.VMEM((slots, tile, tile), jnp.bfloat16),
            pltpu.VMEM((slots, tile, tile), jnp.bfloat16),
            pltpu.VMEM((ITERS + 1, BATCHES) + field, f32),
            pltpu.VMEM(runs + field, f32),
            pltpu.VMEM((BATCHES, tiles, PIECES * batch, tile), jnp.bfloat16),
            pltpu.VMEM((BATCHES, tiles, PIECES * batch, tile), jnp.bfloat16),
            pltpu.VMEM((slots + 1, batch, tile), f32),
            pltpu.VMEM(runs + field, f32),
            pltpu.VMEM(runs + field, f32),
            pltpu.VMEM(runs + half, f32),
            pltpu.VMEM(runs + half, f32),
            pltpu.VMEM(runs + (chips,) + field, f32),
            pltpu.VMEM(runs + (n_col - 1, chunk, batch, LANES), f32),
            pltpu.VMEM((BATCHES,) + field, f32),
            pltpu.VMEM((BATCHES,) + field, f32),
            pltpu.VMEM((3, 2, BATCHES, batch, LANES), f32),
            pltpu.VMEM((3, n_row - 1, 2, BATCHES, batch, LANES), f32),
            dma,
            dma(runs + (chips, CORES)), dma(runs + (CORES,)), dma(runs),
            dma(runs), dma(runs), dma(runs), dma(runs + (chips, CORES)),
            dma(runs + (n_col - 1,)), dma(runs + (n_col - 1,)),
            dma(runs + (n_col - 1,)), dma(runs + (n_col - 1,)),
            dma((3, n_row - 1)), dma((3, n_row - 1)),
        ],
        compiler_params=pltpu.CompilerParams(collective_id=0, has_side_effects=True),
    )(cols, rows, pos, right_sides, nugget.reshape(groups, LANES), cov_blocks[0, 0])
    return start + step * turn, left - step * image


def solution(mesh):
    placed = (
        P(None, ("groups", "row")),
        P(("groups", "row")),
        P(("groups", "row"), "col", None, None, None),
        P(("groups", "row"), "col", None),
        P(("groups", "row"), "col", None),
        P(("groups", "row"), "col"),
    )
    return jax.shard_map(
        functools.partial(on_device, mesh.shape["row"], mesh.shape["col"]),
        mesh=mesh,
        in_specs=placed,
        out_specs=(P(None, ("groups", "row")), P(None, ("groups", "row"))),
        check_vma=False,
    )
```
